32 devices in a mesh: freq: 4 (over y, x), tile: 8 (over z, core).
Axes of the slice: x: 2, y: 2, z: 4, core: 2. Of those that a mesh axis runs over, the one named last changes fastest.
Arguments:
- traces: bfloat16 [256, 8192, 128], P('freq', 'tile'), may hold values from -6 to 6
- right_basis: bfloat16 [16, 8192, 4096], P('freq', 'tile'), may hold values from -0.25 to 0.25
- left_basis: bfloat16 [16, 8192, 4096], P('freq', 'tile'), may hold values from -0.09375 to 0.09375
- tile_ranks: int32 [16, 32, 32], P('freq'), may hold values from 8 to 64, as said below
Outputs:
- wavefield: bfloat16 [16, 2, 8192, 128], P('freq', None, 'tile')
The draws below stay inside these ranges and needn't reach their ends.
Inputs may be any that keep to these rules, and one draw needn't show every extreme that they name: `tile_ranks`: diagonal tiles have rank 64; the ranks of the other tiles are drawn independently of the tile's position, evenly over the whole range.
All inputs are finite; a program needn't handle non-finite values.
Results may differ from the reference program's by a relative error of at most 0.015.
Values may be sent and summed in bfloat16 or wider, within the bound.
A program may use at most 320 MiB of HBM per device.

```python
import math
import jax
import jax.numpy as jnp
from jax import lax

N = 8192
TB = 256
R = 64
S = 128
NF = 16
NT = 256
NB = 32
N_TILE = 8


def draw_tile_ranks(key, part):
    tile_index = jnp.arange(NB, dtype=jnp.int32)
    lowest = max(R // 8, 1)
    rank_value = jax.random.randint(key, (NF, NB, NB), lowest, R + 1, dtype=jnp.int32)
    on_diagonal = tile_index[:, None] == tile_index[None, :]
    rank_value = jnp.where(on_diagonal[None], R, rank_value)
    return rank_value.astype(jnp.int32)


def shard_levels(key, shape, pieces, least, high):
    factor_of, own = 1.0, jax.random.fold_in(key, 6)
    for position, blocks in pieces:
        heights = jnp.exp(jax.random.uniform(jax.random.fold_in(own, position), (blocks,), jnp.float32, least / len(pieces), high / len(pieces)))
        factor_of = factor_of * jnp.repeat(heights, shape[position] // blocks).reshape([-1 if axis == position else 1 for axis in range(len(shape))])
    return factor_of


def normal_values(rng, shape, scale, most, shards=(), kind=jnp.bfloat16):
    result = jax.random.normal(rng, shape, jnp.float32) * scale
    if len(shards) > 0:
        result = shard_levels(rng, shape, shards, -0.22, 0.18) * result
    return jnp.clip(result, min=-most, max=most).astype(kind)


def setup_inputs(seed: int = 0) -> dict:
    key_of = jax.random.split(jax.random.key(seed), 5)
    traces = normal_values(key_of[0], (NT, N, S), 1.0, 6.0, ((0, 4), (1, 8)))
    right_basis = normal_values(key_of[1], (NF, N, 2 * NB * R), (2 * TB) ** -0.5, 0.25, ((0, 4), (1, 8)))
    left_basis = normal_values(key_of[2], (NF, N, 2 * NB * R), (2 * NB * R) ** -0.5, 0.09375, ((0, 4), (1, 8)))
    tile_ranks = draw_tile_ranks(jax.random.fold_in(key_of[4], 71), 0)
    return dict(traces=traces, right_basis=right_basis, left_basis=left_basis, tile_ranks=tile_ranks)


def twiddles(freq_ids, time_ids, total_time):
    phase_int = freq_ids[:, None] * time_ids[None, :] % total_time
    angle_rad = phase_int.astype(jnp.float32) * (2.0 * math.pi / total_time)
    factor = 1.0 / math.sqrt(total_time)
    return jnp.stack([jnp.cos(angle_rad) * factor, -jnp.sin(angle_rad) * factor], 1).astype(jnp.bfloat16)

def reference(traces, right_basis, left_basis, tile_ranks):
    tile_rows = N // TB
    grid_rows = N // N_TILE
    piece_rows = min(TB, grid_rows)
    piece_count = N // piece_rows
    per_tile = max(TB // grid_rows, 1)
    flat_traces = traces.reshape(NT, N * S)
    time_ids = jnp.arange(NT, dtype=jnp.int32)
    column_ids = jnp.arange(piece_count, dtype=jnp.int32) // per_tile

    def one_freq(inputs):
        freq_index, right_freq, left_freq, ranks_freq = inputs
        twiddle = twiddles(jnp.reshape(freq_index + 1, (1,)).astype(jnp.int32), time_ids, NT)[0]
        spectra = jnp.dot(twiddle, flat_traces, preferred_element_type=jnp.float32).astype(jnp.bfloat16)
        spectra = spectra.reshape(2, piece_count, piece_rows, S)
        right_pieces = right_freq.reshape(piece_count, piece_rows, 2 * tile_rows * R)
        products = jnp.einsum('qnc,pqns->cqps', right_pieces.astype(jnp.float32), spectra.astype(jnp.float32))
        products = products.reshape(2, tile_rows, R, piece_count, 2, S)
        real_part = products[0, :, :, :, 0] - products[1, :, :, :, 1]
        imag_part = products[0, :, :, :, 1] + products[1, :, :, :, 0]
        stacked = jnp.transpose(jnp.stack([real_part, imag_part], 0), (3, 1, 0, 2, 4))
        chosen = ranks_freq[:, column_ids]
        keep_rows = jnp.arange(R, dtype=jnp.int32)[None, None, :] < jnp.transpose(chosen)[:, :, None]
        rank_rows = jnp.where(keep_rows[:, :, None, :, None], stacked, jnp.float32(0.0)).astype(jnp.bfloat16)
        grouped = rank_rows.astype(jnp.float32).reshape(tile_rows, per_tile, tile_rows, 2, R, S)
        coupled = lax.optimization_barrier(jnp.sum(grouped, axis=1)).astype(jnp.bfloat16)
        by_row = jnp.transpose(coupled, (1, 0, 2, 3, 4))
        real_coupled = by_row[:, :, 0]
        imag_coupled = by_row[:, :, 1]
        upper_half = jnp.stack([real_coupled, imag_coupled], -2)
        lower_half = jnp.stack([-imag_coupled, real_coupled], -2)
        operand = jnp.stack([upper_half, lower_half], 1)
        left_tiles = left_freq.reshape(tile_rows, TB, 2, tile_rows, R)
        field_out = jnp.einsum('itajk,iajkys->yits', left_tiles.astype(jnp.float32), operand.astype(jnp.float32))
        return field_out.reshape(2, N, S).astype(jnp.bfloat16)
    return lax.map(one_freq, (jnp.arange(NF, dtype=jnp.int32), right_basis, left_basis, tile_ranks))
```

```python
import functools
import math

import jax
import jax.numpy as jnp
from jax import lax
from jax.experimental import pallas as pl
from jax.experimental.pallas import tpu as pltpu
from jax.sharding import PartitionSpec as P


GROUP = 16
VMEM_LIMIT = 60 << 20


def twiddles(freq_ids, time_ids, total_time):
    phase_int = freq_ids[:, None] * time_ids[None, :] % total_time
    angle_rad = phase_int.astype(jnp.float32) * (2.0 * math.pi / total_time)
    factor = 1.0 / math.sqrt(total_time)
    return jnp.stack([jnp.cos(angle_rad) * factor, -jnp.sin(angle_rad) * factor], 1).astype(
        jnp.bfloat16
    )


def send_pieces(rank_rows, tile_count, tile_rows, per_tile):
    freq_dev = rank_rows.shape[1]
    rank_max = rank_rows.shape[4]
    sources = rank_rows.shape[5]
    if tile_rows < tile_count:
        copies = tile_count // tile_rows
        outgoing = jnp.broadcast_to(rank_rows[:, None], (tile_rows, copies) + rank_rows.shape[1:])
        outgoing = outgoing.reshape((tile_count,) + rank_rows.shape[1:])
    else:
        outgoing = rank_rows
    received = lax.all_to_all(outgoing, "tile", split_axis=0, concat_axis=2, tiled=True)
    row_tiles = received.shape[0]
    grouped = received.reshape(row_tiles, freq_dev, tile_rows, per_tile, 2, rank_max, sources)
    return jnp.sum(grouped.astype(jnp.float32), axis=3).astype(jnp.bfloat16)


def plain_body(traces, right_basis, left_basis, tile_ranks, first, stride):
    freq_count = lax.axis_size("freq")
    tile_count = lax.axis_size("tile")
    time_rows, grid_rows, sources = traces.shape
    freq_dev = right_basis.shape[0]
    total_time = time_rows * freq_count
    tile_rows = tile_ranks.shape[1]
    rank_max = right_basis.shape[2] // (2 * tile_rows)
    tile_points = grid_rows * tile_count // tile_rows
    freq_ids = (
        1
        + jnp.arange(freq_count, dtype=jnp.int32)[:, None] * stride
        + (first + jnp.arange(freq_dev, dtype=jnp.int32))[None, :]
    ).reshape(freq_count * freq_dev)
    time_ids = lax.axis_index("freq") * time_rows + jnp.arange(time_rows, dtype=jnp.int32)
    twiddle = twiddles(freq_ids, time_ids, total_time)
    partial_sums = jnp.einsum(
        "fpt,tns->fpns", twiddle, traces, preferred_element_type=jnp.float32
    ).astype(jnp.bfloat16)
    shares = lax.all_to_all(partial_sums, "freq", split_axis=0, concat_axis=0, tiled=True)
    shares = shares.reshape((freq_count, freq_dev) + shares.shape[1:])
    spectra = jnp.sum(shares.astype(jnp.float32), axis=0).astype(jnp.bfloat16)
    piece_rows = min(tile_points, grid_rows)
    pieces_dev = grid_rows // piece_rows
    per_tile = max(tile_points // grid_rows, 1)
    spectra_pieces = spectra.reshape(freq_dev, 2, pieces_dev, piece_rows, sources)
    right_pieces = right_basis.reshape(freq_dev, pieces_dev, piece_rows, 2 * tile_rows * rank_max)
    products = jnp.einsum(
        "fqnc,fpqns->cfqps", right_pieces, spectra_pieces, preferred_element_type=jnp.float32
    )
    products = products.reshape(2, tile_rows, rank_max, freq_dev, pieces_dev, 2, sources)
    real_part = products[0, :, :, :, :, 0] - products[1, :, :, :, :, 1]
    imag_part = products[0, :, :, :, :, 1] + products[1, :, :, :, :, 0]
    stacked = jnp.transpose(jnp.stack([real_part, imag_part], 0), (1, 3, 4, 0, 2, 5))
    column_ids = (
        lax.axis_index("tile") * pieces_dev + jnp.arange(pieces_dev, dtype=jnp.int32)
    ) // per_tile
    onehot = (column_ids[:, None] == jnp.arange(tile_rows, dtype=jnp.int32)[None, :]).astype(
        jnp.int32
    )
    chosen = jnp.sum(tile_ranks[:, :, None, :] * onehot[None, None], axis=-1)
    keep_rows = jnp.arange(rank_max, dtype=jnp.int32)[None, None, None, :] < chosen[..., None]
    keep_rows = jnp.transpose(keep_rows, (1, 0, 2, 3))[:, :, :, None, :, None]
    rank_rows = jnp.where(keep_rows, stacked, jnp.float32(0.0)).astype(jnp.bfloat16)
    coupled = send_pieces(rank_rows, tile_count, tile_rows, per_tile)
    row_tiles = coupled.shape[0]
    rows_tile = grid_rows // row_tiles
    real_coupled = coupled[:, :, :, 0]
    imag_coupled = coupled[:, :, :, 1]
    upper_half = jnp.stack([real_coupled, imag_coupled], -2)
    lower_half = jnp.stack([-imag_coupled, real_coupled], -2)
    operand = jnp.stack([upper_half, lower_half], 2)
    left_tiles = left_basis.reshape(freq_dev, row_tiles, rows_tile, 2, tile_rows, rank_max)
    field_out = jnp.einsum(
        "frtajk,rfajkys->fyrts", left_tiles, operand, preferred_element_type=jnp.float32
    )
    return field_out.reshape(freq_dev, 2, grid_rows, sources).astype(jnp.bfloat16)


def plain_scan(traces, right_basis, left_basis, tile_ranks):
    freq_dev = right_basis.shape[0]

    def one(carry, first):
        def pick(array):
            return lax.dynamic_slice_in_dim(array, first, 1, axis=0)

        field = plain_body(
            traces, pick(right_basis), pick(left_basis), pick(tile_ranks), first, freq_dev
        )
        return carry, field[0]

    return lax.scan(one, 0, jnp.arange(freq_dev, dtype=jnp.int32))[1]


def dft_kernel(rows, tw_ref, x_ref, *refs):
    outs, weights = refs[:-1], refs[-1]
    times, block, sources = x_ref.shape

    @pl.when(pl.program_id(0) == 0)
    def _():
        spread = lax.broadcasted_iota(jnp.int32, (times, times * GROUP), 1) // GROUP
        spread = spread == lax.broadcasted_iota(jnp.int32, (times, times * GROUP), 0)
        wide = jnp.dot(
            tw_ref[...], jnp.where(spread, 1.0, 0.0).astype(jnp.bfloat16),
            preferred_element_type=jnp.float32,
        )
        row = lax.broadcasted_iota(jnp.int32, (GROUP, times * GROUP), 0)
        col = lax.broadcasted_iota(jnp.int32, (GROUP, times * GROUP), 1) % GROUP
        for q in range(rows):
            line = jnp.broadcast_to(wide[q : q + 1], (GROUP, times * GROUP))
            weights[q * GROUP : (q + 1) * GROUP, :] = jnp.where(row == col, line, 0.0).astype(
                jnp.bfloat16
            )

    @pl.loop(0, block // (2 * GROUP), unroll=True)
    def _(pair):
        starts = [pl.multiple_of(pair * 2 * GROUP + h * GROUP, GROUP) for h in range(2)]
        halves = [
            x_ref[:, pl.ds(start, GROUP), :].reshape(times * GROUP, sources) for start in starts
        ]
        total = jnp.dot(
            weights[...], jnp.concatenate(halves, axis=1), preferred_element_type=jnp.float32
        ).astype(jnp.bfloat16)
        for q in range(rows):
            for h in range(2):
                outs[q // 2][q % 2, pl.ds(starts[h], GROUP), :] = total[
                    q * GROUP : (q + 1) * GROUP, h * sources : (h + 1) * sources
                ]


def dft(slots, point_range, freq_dev, traces):
    freq_count = lax.axis_size("freq")
    me = lax.axis_index("freq")
    time_rows, _, sources = traces.shape
    first, last = point_range
    points = last - first
    block = min(128, points)
    owners = (me + jnp.arange(freq_count, dtype=jnp.int32)) % freq_count
    ids = 1 + owners[None, :] * freq_dev + jnp.asarray(slots, jnp.int32)[:, None]
    time_ids = me * time_rows + jnp.arange(time_rows, dtype=jnp.int32)
    table = twiddles(ids.reshape(-1), time_ids, time_rows * freq_count)
    rows = 2 * len(slots) * freq_count
    outs = pl.pallas_call(
        functools.partial(dft_kernel, rows),
        out_shape=[jax.ShapeDtypeStruct((2, points, sources), jnp.bfloat16)] * (rows // 2),
        grid=(points // block,),
        in_specs=[
            pl.BlockSpec((rows, time_rows), lambda n: (0, 0)),
            pl.BlockSpec((time_rows, block, sources), lambda n: (0, n + first // block, 0)),
        ],
        out_specs=[pl.BlockSpec((2, block, sources), lambda n: (0, n, 0))] * (rows // 2),
        scratch_shapes=[pltpu.VMEM((rows * GROUP, time_rows * GROUP), jnp.bfloat16)],
        compiler_params=pltpu.CompilerParams(vmem_limit_bytes=VMEM_LIMIT),
        cost_estimate=pl.CostEstimate(
            flops=2 * rows * GROUP * time_rows * points * sources,
            bytes_accessed=2 * time_rows * points * sources + 2 * rows * points * sources,
            transcendentals=0,
        ),
        name="partial_spectra",
    )(table.reshape(rows, time_rows), traces)
    return [outs[n * freq_count : (n + 1) * freq_count] for n in range(len(slots))]


def share_out(parts):
    freq_count = len(parts)
    received = [parts[0]]
    for k in range(1, freq_count):
        ring = [(i, (i + k) % freq_count) for i in range(freq_count)]
        received.append(lax.ppermute(parts[k], "freq", ring))
    return received


def pack_kernel(dims, plan, off_ref, rank_ref, place_ref, *refs):
    chips, rows_chip, rank, sources, tiles = dims
    first, cuts, carry_in, carry_out, full, shares = plan
    length = cuts[-1]
    pieces = list(zip(cuts[:-1], cuts[1:]))
    share_refs, refs = refs[:shares], refs[shares:]
    right_ref, refs = refs[0], refs[1:]
    if carry_in:
        carried_ref, refs = refs[0], refs[1:]
    sent = len(pieces) * (chips - 1)
    out_refs, refs = refs[:sent], refs[sent:]
    own_ref, refs = refs[0], refs[1:]
    if carry_out:
        carry_ref, refs = refs[0], refs[1:]
    (buf,) = refs
    unit = pl.program_id(0)
    half = chips * rows_chip * rank
    chip = place_ref[0]

    if carry_in:

        @pl.when(unit == 0)
        def _():
            for dest in range(chips):
                for part in range(2):
                    lanes = slice(part * sources, (part + 1) * sources)
                    buf[part, dest, :carry_in, :] = carried_ref[dest, :, lanes].astype(jnp.float32)

    spectra = share_refs[0][...].astype(jnp.float32)
    for ref in share_refs[1:]:
        spectra = spectra + ref[...].astype(jnp.float32)
    spectra = spectra.astype(jnp.bfloat16)
    real, imag = spectra[0], spectra[1]
    upper = jnp.concatenate([real, imag], axis=1)
    lower = jnp.concatenate([-imag, real], axis=1)
    rows = lax.broadcasted_iota(jnp.int32, (rank, 2 * sources), 0)
    contract = (((0,), (0,)), ((), ()))
    width = rows_chip * rank
    for dest in range(chips):
        real_cols = right_ref[0, :, dest * width : (dest + 1) * width]
        imag_cols = right_ref[0, :, half + dest * width : half + (dest + 1) * width]
        total = lax.dot_general(real_cols, upper, contract, preferred_element_type=jnp.float32)
        total += lax.dot_general(imag_cols, lower, contract, preferred_element_type=jnp.float32)
        for row in range(rows_chip):
            index = dest * tiles + (first + unit) * rows_chip + row
            kept = jnp.where(rows < rank_ref[index], total[row * rank : (row + 1) * rank], 0.0)
            buf[0, dest, pl.ds(off_ref[index], rank), :] = kept[:, :sources]
            buf[1, dest, pl.ds(off_ref[index], rank), :] = kept[:, sources:]

    @pl.when(unit == pl.num_programs(0) - 1)
    def _():
        for part in range(2):
            lanes = slice(part * sources, (part + 1) * sources)
            for k in range(1, chips):
                dest = lax.rem(chip + k, chips)
                for n, (a, b) in enumerate(pieces):
                    out_refs[n * (chips - 1) + k - 1][:, lanes] = buf[part, dest, a:b, :].astype(
                        jnp.bfloat16
                    )
            own_ref[:, lanes] = buf[part, chip, :full, :].astype(jnp.bfloat16)
            if carry_out:
                for dest in range(chips):
                    carry_ref[dest, :, lanes] = buf[part, dest, length : length + carry_out, :].astype(
                        jnp.bfloat16
                    )


def pack(dims, chunk, tables, shares, base, right_basis, carried):
    chips, rows_chip, rank, sources, tiles = dims
    first, count, cuts, carry_in, carry_out = chunk
    length = cuts[-1]
    sizes = [b - a for a, b in zip(cuts[:-1], cuts[1:]) for _ in range(chips - 1)]
    freq_dev, grid_rows, width = right_basis.shape
    per_freq = tiles // rows_chip // freq_dev
    points = grid_rows // per_freq
    full = count * rows_chip * rank
    space = max(length + carry_out, full) + rank
    in_specs = [
        pl.BlockSpec((2, points, sources), lambda u, *_: (0, (first + u) % per_freq - base, 0))
    ] * len(shares)
    in_specs += [
        pl.BlockSpec(
            (1, points, width), lambda u, *_: ((first + u) // per_freq, (first + u) % per_freq, 0)
        )
    ]
    out_shape = [jax.ShapeDtypeStruct((size, 2 * sources), jnp.bfloat16) for size in sizes]
    out_shape += [jax.ShapeDtypeStruct((full, 2 * sources), jnp.bfloat16)]
    out_specs = [pl.BlockSpec((size, 2 * sources), lambda u, *_: (0, 0)) for size in sizes]
    out_specs += [pl.BlockSpec((full, 2 * sources), lambda u, *_: (0, 0))]
    inputs = [*shares, right_basis]
    if carry_in:
        shape = (chips, carry_in, 2 * sources)
        in_specs += [pl.BlockSpec(shape, lambda u, *_: (0, 0, 0))]
        inputs += [carried]
    if carry_out:
        shape = (chips, carry_out, 2 * sources)
        out_shape += [jax.ShapeDtypeStruct(shape, jnp.bfloat16)]
        out_specs += [pl.BlockSpec(shape, lambda u, *_: (0, 0, 0))]
    plan = (first, cuts, carry_in, carry_out, full, len(shares))
    outs = pl.pallas_call(
        functools.partial(pack_kernel, dims, plan),
        out_shape=out_shape,
        grid_spec=pltpu.PrefetchScalarGridSpec(
            num_scalar_prefetch=3,
            grid=(count,),
            in_specs=in_specs,
            out_specs=out_specs,
            scratch_shapes=[pltpu.VMEM((2, chips, space, sources), jnp.float32)],
        ),
        compiler_params=pltpu.CompilerParams(vmem_limit_bytes=VMEM_LIMIT),
        cost_estimate=pl.CostEstimate(
            flops=4 * count * points * width * sources,
            bytes_accessed=2 * count * points * width + 4 * chips * space * sources,
            transcendentals=0,
        ),
        name="pack_rows",
    )(*tables, *inputs)
    sent = len(sizes)
    return list(outs[:sent]), outs[sent], outs[sent + 1] if carry_out else None


def apply_kernel(dims, plan, off_ref, rank_ref, place_ref, *refs):
    chips, rows_chip, rank, sources, tiles = dims
    freq, per_freq, per_dev, layout, has_field = plan
    count = sum(len(spans) for spans in layout)
    seg_refs, refs = refs[:count], refs[count:]
    left_ref, refs = refs[0], refs[1:]
    if has_field:
        refs = refs[1:]
    out_ref, buf, operand = refs
    row = pl.program_id(0)
    chip, core = place_ref[0], place_ref[1]
    half = 2 * chips * per_dev * rank

    @pl.when(row == 0)
    def _():
        at = 0
        for source, spans in enumerate(layout):
            for start, length in spans:
                for part in range(2):
                    lanes = slice(part * sources, (part + 1) * sources)
                    buf[part, source, start : start + length, :] = seg_refs[at][:, lanes].astype(
                        jnp.float32
                    )
                at += 1

    rows = lax.broadcasted_iota(jnp.int32, (rank, sources), 0)
    for source in range(len(layout)):
        k, other = source // 2, source % 2
        lane_core = core if other == 0 else 1 - core
        device = 2 * lax.rem(chip + chips - k, chips) + lane_core
        for each in range(per_dev):
            index = device * tiles + (freq * per_freq + each) * rows_chip + core * per_dev + row
            col = device * per_dev + each
            window = pl.ds(off_ref[index], rank)
            keep = rows < rank_ref[index]
            real = jnp.where(keep, buf[0, source, window, :], 0.0)
            imag = jnp.where(keep, buf[1, source, window, :], 0.0)
            upper = pl.ds(pl.multiple_of(col * rank, rank), rank)
            lower = pl.ds(pl.multiple_of(half + col * rank, rank), rank)
            operand[upper, :sources] = real.astype(operand.dtype)
            operand[upper, sources:] = imag.astype(operand.dtype)
            operand[lower, :sources] = (-imag).astype(operand.dtype)
            operand[lower, sources:] = real.astype(operand.dtype)

    field = jnp.dot(left_ref[0], operand[...], preferred_element_type=jnp.float32)
    out_ref[0, 0] = field[:, :sources].astype(out_ref.dtype)
    out_ref[0, 1] = field[:, sources:].astype(out_ref.dtype)


def apply_left(dims, freq, per_dev, tables, segments, left_basis, field):
    chips, rows_chip, rank, sources, tiles = dims
    freq_dev, grid_rows, width = left_basis.shape
    points = grid_rows // per_dev
    layout, arrays, in_specs = [], [], []
    for spans in segments:
        layout.append(tuple((start, length) for start, length, _ in spans))
        for _, length, array in spans:
            arrays.append(array)
            in_specs.append(pl.BlockSpec((length, 2 * sources), lambda i, *_: (0, 0)))
    space = max(start + length for spans in layout for start, length in spans) + rank
    in_specs.append(pl.BlockSpec((1, points, width), lambda i, *_: (freq, i, 0)))
    arrays.append(left_basis)
    aliases = {}
    if field is not None:
        aliases = {3 + len(arrays): 0}
        in_specs.append(pl.BlockSpec(memory_space=pl.ANY))
        arrays.append(field)
    plan = (freq, tiles // rows_chip // freq_dev, per_dev, tuple(layout), field is not None)
    return pl.pallas_call(
        functools.partial(apply_kernel, dims, plan),
        out_shape=jax.ShapeDtypeStruct((freq_dev, 2, grid_rows, sources), jnp.bfloat16),
        grid_spec=pltpu.PrefetchScalarGridSpec(
            num_scalar_prefetch=3,
            grid=(per_dev,),
            in_specs=in_specs,
            out_specs=pl.BlockSpec((1, 2, points, sources), lambda i, *_: (freq, 0, i, 0)),
            scratch_shapes=[
                pltpu.VMEM((2, 2 * chips, space, sources), jnp.float32),
                pltpu.VMEM((width, 2 * sources), jnp.bfloat16),
            ],
        ),
        input_output_aliases=aliases,
        compiler_params=pltpu.CompilerParams(vmem_limit_bytes=VMEM_LIMIT),
        cost_estimate=pl.CostEstimate(
            flops=4 * grid_rows * width * sources,
            bytes_accessed=2 * grid_rows * width + 8 * chips * space * sources,
            transcendentals=0,
        ),
        name="apply_left",
    )(*tables, *arrays)


def up16(value):
    return -(-int(value) // 16) * 16


def make_plan(groups, rows_chip, rank):
    lowest = max(rank // 8, 1)
    mean = (lowest + rank) / 2
    spread = math.sqrt(((rank - lowest + 1) ** 2 - 1) / 12)
    chunks, start, done = [], 0, 0
    for n, count in enumerate(groups):
        total = (done + count) * rows_chip
        deviation = spread * math.sqrt(total)
        if n + 1 < len(groups):
            end = max(int(mean * total - deviation) // 16 * 16, start + 16)
            carry = up16(mean * total + 4.1 * deviation) - end
        else:
            end, carry = max(up16(mean * total + 4.1 * deviation), start + 16), 0
        chunks.append((done, count, start, end - start, carry))
        start, done = end, done + count
    return chunks


def make_tables(chunks, tile_ranks, chips, rows_chip, per_dev, rank):
    freq_dev = tile_ranks.shape[0]
    tiles = freq_dev * per_dev * rows_chip
    peers = 2 * chips
    split = tile_ranks.reshape(freq_dev, chips, rows_chip, peers, per_dev)
    ranks = jnp.transpose(split, (3, 1, 0, 4, 2)).reshape(peers, chips, tiles)
    tile = jnp.arange(tiles, dtype=jnp.int32)
    bounds = [0] + [(first + count) * rows_chip for first, count, *_ in chunks]
    member = sum((tile >= bound).astype(jnp.int32) for bound in bounds[1:-1]) + 0 * tile
    before = (tile[:, None] < tile[None, :]) & (member[:, None] == member[None, :])
    exact = ranks.astype(jnp.bfloat16)
    within = jnp.einsum(
        "abt,tu->abu", exact, before.astype(jnp.bfloat16), preferred_element_type=jnp.float32
    ).astype(jnp.int32)
    belongs = member[:, None] == jnp.arange(len(chunks), dtype=jnp.int32)[None, :]
    totals = jnp.einsum(
        "abt,tc->abc", exact, belongs.astype(jnp.bfloat16), preferred_element_type=jnp.float32
    ).astype(jnp.int32)
    end = jnp.zeros((peers, chips), jnp.int32)
    over = jnp.zeros((peers, chips), bool)
    base = jnp.zeros((peers, chips, tiles), jnp.int32)
    for n, (_, _, start, length, carry) in enumerate(chunks):
        begin = jnp.maximum(end, start)
        end = begin + totals[:, :, n]
        over = over | (end > start + length + carry)
        base = jnp.where(member == n, begin[:, :, None], base)
    source_chip = jnp.arange(peers, dtype=jnp.int32)[:, None] // 2
    over = jnp.any(over & (source_chip != jnp.arange(chips, dtype=jnp.int32)[None, :]))
    place = base + within
    sent_start, sent_limit, sent_own, got_start, got_limit, got_own = [], [], [], [], [], []
    per_freq = per_dev
    for first, count, start, length, carry in chunks:
        for unit in range(first, first + count):
            freq = unit // per_freq
            members = [c for c in chunks if c[0] < (freq + 1) * per_freq and c[0] + c[1] > freq * per_freq]
            origin = members[0][2]
            limit = members[-1][2] + members[-1][3] + members[-1][4] - origin
            for row in range(rows_chip):
                sent_start.append(start)
                sent_limit.append(length + carry)
                sent_own.append(((unit - first) * rows_chip + row) * rank)
                got_start.append(origin)
                got_limit.append(limit)
                got_own.append(((unit % per_freq) * rows_chip + row) * rank)

    def row(values):
        return jnp.asarray(values, jnp.int32)[None, :]

    me = lax.axis_index("tile")
    chip = me // 2
    sent = lax.dynamic_index_in_dim(place, me, 0, keepdims=False)
    got = lax.dynamic_index_in_dim(place, chip, 1, keepdims=False)
    sent = jnp.clip(sent - row(sent_start), 0, row(sent_limit))
    got = jnp.clip(got - row(got_start), 0, row(got_limit))
    sent = jnp.where(jnp.arange(chips)[:, None] == chip, row(sent_own), sent)
    got = jnp.where(jnp.arange(peers)[:, None] // 2 == chip, row(got_own), got)
    sent_ranks = lax.dynamic_index_in_dim(ranks, me, 0, keepdims=False)
    got_ranks = lax.dynamic_index_in_dim(ranks, chip, 1, keepdims=False)
    where = jnp.stack([chip, me % 2]).astype(jnp.int32)
    sending = (sent.reshape(-1), sent_ranks.reshape(-1), where)
    receiving = (got.reshape(-1), got_ranks.reshape(-1), where)
    return sending, receiving, over


def body(traces, right_basis, left_basis, tile_ranks):
    peers = lax.axis_size("tile")
    freq_count = lax.axis_size("freq")
    tile_rows = tile_ranks.shape[1]
    freq_dev, grid_rows, width = right_basis.shape
    if tile_rows % peers != 0 or peers % 2 != 0 or freq_dev < 2 or grid_rows % 128 != 0:
        return plain_body(traces, right_basis, left_basis, tile_ranks, 0, freq_dev)
    sources = traces.shape[2]
    chips = peers // 2
    per_dev = tile_rows // peers
    rows_chip = 2 * per_dev
    rank = width // (2 * tile_rows)
    tiles = freq_dev * per_dev * rows_chip
    dims = (chips, rows_chip, rank, sources, tiles)
    groups = [per_dev] * freq_dev
    chunks = make_plan(groups, rows_chip, rank)

    head = dft([0], (0, grid_rows), freq_dev, traces)
    shares = [share_out(head[0])]
    rest = dft(list(range(1, freq_dev)), (0, grid_rows), freq_dev, traces)
    shares += [share_out(parts) for parts in rest]
    sending, receiving, over = make_tables(chunks, tile_ranks, chips, rows_chip, per_dev, rank)

    flag = jnp.broadcast_to(jnp.where(over, 1.0, 0.0).astype(jnp.float32), (8, 128))
    total = flag
    for k in range(1, freq_count):
        ring = [(i, (i + k) % freq_count) for i in range(freq_count)]
        total = total + lax.ppermute(flag, "freq", ring)
    over = total[0, 0] > 0.5

    def turn(k):
        return [(2 * z + c, 2 * ((z + k) % chips) + c) for z in range(chips) for c in range(2)]

    swap = [(i, i ^ 1) for i in range(peers)]
    carried, carry_in = None, 0
    got, own = [], []
    for n, (first, count, start, length, carry) in enumerate(chunks):
        cuts = (0, length)
        if n + 1 == len(chunks):
            cuts = (0, length * 3 // 4 // 16 * 16, length)
        sent, mine, carried = pack(
            dims, (first, count, cuts, carry_in, carry), sending, shares[n], 0, right_basis, carried
        )
        carry_in = carry
        for a, b in zip(cuts[:-1], cuts[1:]):
            straight, crossed = [], []
            for k in range(1, chips):
                straight.append(lax.ppermute(sent.pop(0), "tile", turn(k)))
                crossed.append(lax.ppermute(straight[-1], "tile", swap))
            got.append((start + a, b - a, straight, crossed))
        own.append((mine, lax.ppermute(mine, "tile", swap)))

    def segments(n):
        _, count, start, length, carry = chunks[n]
        full = count * rows_chip * rank
        result = [[(0, full, own[n][0])], [(0, full, own[n][1])]]
        for k in range(1, chips):
            for side in range(2):
                spans = []
                for at, rows, *pieces in got:
                    used = min(at + rows, start + length + carry) - at
                    if at >= start and used > 0:
                        spans.append((at - start, used, pieces[side][k - 1]))
                result.append(spans)
        return result

    field = None
    for n in range(freq_dev - 1):
        field = apply_left(dims, n, per_dev, receiving, segments(n), left_basis, field)

    def fast(field, receiving, pieces, traces, right_basis, left_basis, tile_ranks):
        spans = [
            [(start, rows, array) for (start, rows, _), array in zip(old, new)]
            for old, new in zip(segments(freq_dev - 1), pieces)
        ]
        return apply_left(dims, freq_dev - 1, per_dev, receiving, spans, left_basis, field)

    def complete(field, receiving, pieces, traces, right_basis, left_basis, tile_ranks):
        return plain_scan(traces, right_basis, left_basis, tile_ranks)

    pieces = [[array for _, _, array in spans] for spans in segments(freq_dev - 1)]
    return lax.cond(
        over, complete, fast, field, receiving, pieces, traces, right_basis, left_basis, tile_ranks
    )


def solution(mesh):
    return jax.shard_map(
        body,
        mesh=mesh,
        in_specs=(
            P("freq", "tile", None),
            P("freq", "tile", None),
            P("freq", "tile", None),
            P("freq", None, None),
        ),
        out_specs=P("freq", None, "tile", None),
        check_vma=False,
    )
```
